32 devices in a mesh: dp: 4 (over y, x), seq: 8 (over z, core).
Axes of the slice: x: 2, y: 2, z: 4, core: 2. Of those that a mesh axis runs over, the one named last changes fastest.
Arguments:
- tokens: bfloat16 [8192, 5120], P(('dp', 'seq')), may hold values from -6 to 6
- cotangent: bfloat16 [8192, 5120], P(('dp', 'seq')), may hold values from -6 to 6
- arrival_slot: int32 [4, 8, 8], P('dp'), may hold values from 0 to 7, as said below
- valid_count: int32 [4, 8], P('dp'), may hold values from 0 to 256
- doc_lengths: int32 [4, 8], P('dp'), may hold values from 1 to 1024, 2048 in all within a row
- gate_a: bfloat16 [5120, 320], P('dp'), may hold values from -0.3125 to 0.3125
- gate_x: bfloat16 [5120, 320], P('dp'), may hold values from -0.3125 to 0.3125
- decay_param: float32 [5120], replicated, as said below
Outputs:
- states_out: bfloat16 [8192, 5120], P(('dp', 'seq'))
- token_grad: bfloat16 [8192, 5120], P(('dp', 'seq'))
- grad_gate_a: float32 [5120, 320], P(('dp', 'seq'))
- grad_gate_x: float32 [5120, 320], P(('dp', 'seq'))
- grad_decay: float32 [5120], P(('dp', 'seq'))
The draws below stay inside these ranges and needn't reach their ends.
Inputs may be any that keep to these rules, and one draw needn't show every extreme that they name: For each group p and each owner k, arrival_slot[p, s, k] over the 8 loading devices s is a permutation of 0 to 7. decay_param lies between 4.6 and ln(2048) + 2.
All inputs are finite; a program needn't handle non-finite values.
Results may differ from the reference program's by a relative error of at most 0.0026.
Values may be sent and summed in bfloat16 or wider, within the bound.
No kernel may reach another device: no remote copies, remote signals or barrier semaphores. Data moves between devices by JAX's collectives and lax.ppermute only.
A program may use at most 192 MiB of HBM per device.

```python
import math
import jax
import jax.numpy as jnp
import numpy as np
from jax import lax

R = 5120
H = 16
TOK_DEV = 256
NDOC = 8
HS = 320
BLK = 32
GROUP_TOK = 2048
TOKENS = 8192
N_DP = 4
N_SEQ = 8


def draw_arrival_slot(key, part):
    key_list = jax.random.split(key, N_DP * N_SEQ)
    orders = jax.vmap(lambda one_key: jax.random.permutation(one_key, N_SEQ))(key_list)
    orders = orders.reshape(N_DP, N_SEQ, N_SEQ)
    return jnp.swapaxes(orders, 1, 2).astype(jnp.int32)


def draw_decay_param(key, part):
    key_slow, key_fast, key_pick = jax.random.split(key, 3)
    slow_value = jnp.log(jnp.float32(GROUP_TOK)) + jax.random.uniform(key_slow, (R,), jnp.float32, 0.6, 2.0)
    fast_value = jax.random.uniform(key_fast, (R,), jnp.float32, 4.6, 5.1)
    keep_share = 0.5
    slow_pick = jax.random.uniform(key_pick, (R,), jnp.float32) < keep_share
    return jnp.where(slow_pick, slow_value, fast_value).astype(jnp.float32)


def with_ends(result, own_key, low, top_value):
    longest = result.shape.index(max(result.shape))
    spots = []
    for shift in (0, 1):
        where = [jax.random.randint(jax.random.fold_in(own_key, axis), (), 0, length) for axis, length in enumerate(result.shape)]
        where[longest] = (where[longest] + shift) % result.shape[longest]
        spots.append(tuple(where))
    return result.at[spots[0]].set(low).at[spots[1]].set(top_value)


def steps_of(rng, extent, shards, least, high):
    factor_of, own = 1.0, jax.random.fold_in(rng, 6)
    for dim, shards_of in shards:
        draws = jnp.exp(jax.random.uniform(jax.random.fold_in(own, dim), (shards_of,), jnp.float32, least / len(shards), high / len(shards)))
        factor_of = factor_of * jnp.repeat(draws, extent[dim] // shards_of).reshape([-1 if axis == dim else 1 for axis in range(len(extent))])
    return factor_of


def profile(count, total, bound, lean):
    portions = [(1 << 20) // math.isqrt(standing ** lean) + 1 for standing in range(2, count + 1)]
    spare, given = total - bound - (count - 1), [1] * (count - 1)
    while spare > 0:
        candidates = [i for i in range(count - 1) if given[i] < bound]
        whole, left = sum([portions[i] for i in candidates]), spare
        for i in candidates:
            extra = min(bound - given[i], max(1, left * portions[i] // whole), spare)
            given[i] = given[i] + extra
            spare = spare - extra
    return np.array([bound] + given)


def uneven(rng, number_of, total, most, slope):
    if number_of == 2:
        one = jax.random.randint(rng, (), max(1, total - most), min(most, total - 1) + 1)
        return jnp.stack([one, total - one])
    sizes = jnp.asarray(profile(number_of, total, most, slope), jnp.int32)
    twos = (number_of - 1) // 2
    source_of, sink = sizes[1:1 + 2 * twos:2], sizes[2:2 + 2 * twos:2]
    margin = jnp.minimum(source_of - 1, most - sink)
    passed = jax.random.randint(jax.random.fold_in(rng, 1), (twos,), 0, 1 << 20) % (margin + 1)
    sizes = sizes.at[1:1 + 2 * twos:2].set(source_of - passed).at[2:2 + 2 * twos:2].set(sink + passed)
    return sizes[jax.random.permutation(jax.random.fold_in(rng, 2), number_of)]


def normal_values(rng, extent, width, most, shards=(), kind=jnp.bfloat16):
    array = jax.random.normal(rng, extent, jnp.float32) * width
    if len(shards) > 0:
        array = steps_of(rng, extent, shards, -0.22, 0.18) * array
    return jnp.clip(array, min=-most, max=most).astype(kind)


def setup_inputs(seed: int = 0) -> dict:
    key_of = jax.random.split(jax.random.key(seed), 9)
    tokens = normal_values(key_of[0], (TOKENS, R), 1.0, 6.0, ((0, 32),))
    cotangent = normal_values(key_of[1], (TOKENS, R), 1.0, 6.0, ((0, 32),))
    arrival_slot = draw_arrival_slot(jax.random.fold_in(key_of[8], 71), 0)
    valid_count = with_ends(jax.random.randint(key_of[3], (N_DP, N_SEQ), 0, TOK_DEV + 1), jax.random.fold_in(key_of[3], 1), 0, TOK_DEV).astype(jnp.int32)
    doc_lengths = jax.vmap(lambda own: uneven(own, NDOC, GROUP_TOK, GROUP_TOK // 2, 2))(jax.random.split(key_of[4], N_DP)).reshape((N_DP, NDOC)).astype(jnp.int32)
    gate_a = normal_values(key_of[5], (R, HS), HS ** -0.5, 0.3125, ((0, 4),))
    gate_x = normal_values(key_of[6], (R, HS), HS ** -0.5, 0.3125, ((0, 4),))
    decay_param = draw_decay_param(jax.random.fold_in(key_of[8], 71), 0)
    return dict(tokens=tokens, cotangent=cotangent, arrival_slot=arrival_slot, valid_count=valid_count, doc_lengths=doc_lengths, gate_a=gate_a, gate_x=gate_x, decay_param=decay_param)


SHARP = 8.0

def head_product(token_rows, weight):
    row_blocks = token_rows.reshape(-1, H, HS).astype(jnp.float32)
    weight_blocks = weight.reshape(H, HS, HS).astype(jnp.float32)
    return jnp.einsum('thc,hcd->thd', row_blocks, weight_blocks).reshape(-1, R)

def head_back(grad_rows, weight):
    grad_blocks = grad_rows.reshape(-1, H, HS).astype(jnp.float32)
    weight_blocks = weight.reshape(H, HS, HS).astype(jnp.float32)
    return jnp.einsum('thd,hcd->thc', grad_blocks, weight_blocks).reshape(-1, R)

def head_outer(token_rows, grad_rows):
    row_blocks = token_rows.reshape(-1, H, HS).astype(jnp.float32)
    grad_blocks = grad_rows.reshape(-1, H, HS).astype(jnp.float32)
    return jnp.einsum('thc,thd->hcd', row_blocks, grad_blocks).reshape(R, HS)

def to_bucket(loaded, slot_table):
    pieces = jnp.swapaxes(loaded.reshape(N_SEQ, N_SEQ, BLK, R), 0, 1)
    slot_iota = jnp.arange(N_SEQ, dtype=jnp.int32)
    slot_match = slot_table[:, :, None] == slot_iota[None, None, :]
    source = lax.optimization_barrier(jnp.sum(jnp.where(slot_match, slot_iota[:, None, None], 0), axis=0)).astype(jnp.int32)
    ordered = jax.vmap(lambda piece_set, slot_picks: piece_set[slot_picks])(pieces, source)
    return ordered.reshape(GROUP_TOK, R)

def to_loader(bucket, slot_table):
    pieces = bucket.reshape(N_SEQ, N_SEQ, BLK, R)
    picked = jax.vmap(lambda piece_set, slot_picks: piece_set[slot_picks])(pieces, jnp.swapaxes(slot_table, 0, 1))
    return jnp.swapaxes(picked, 0, 1).reshape(GROUP_TOK, R)

def reference(tokens, cotangent, arrival_slot, valid_count, doc_lengths, gate_a, gate_x, decay_param):

    def one_group(operands):
        loaded_rows, loaded_grads, slot_table, counts, lengths = operands
        token_rows = to_bucket(loaded_rows, slot_table)
        out_grads = to_bucket(loaded_grads, slot_table)
        positions = jnp.arange(GROUP_TOK, dtype=jnp.int32)
        starts = (jnp.cumsum(lengths) - lengths).astype(jnp.int32)
        doc_start = jnp.any(positions[:, None] == starts[None, :], axis=1)
        keep_mask = jnp.where(doc_start, 0.0, 1.0).astype(jnp.float32)[:, None]
        owner_count = counts[positions // TOK_DEV]
        loss_mask = jnp.where(positions % TOK_DEV < owner_count, 1.0, 0.0).astype(jnp.float32)[:, None]
        gate_rate = jax.nn.sigmoid(head_product(token_rows, gate_a))
        gate_inlet = jax.nn.sigmoid(head_product(token_rows, gate_x))
        soft_decay = jax.nn.softplus(-decay_param)
        log_decay = -SHARP * gate_rate * soft_decay
        decay_factor = jnp.exp(log_decay)
        carry_mul = decay_factor * keep_mask
        input_scale = keep_mask * jnp.sqrt(-jnp.expm1(2.0 * log_decay)) + (1.0 - keep_mask)
        row_values = token_rows.astype(jnp.float32)
        drive_term = input_scale * gate_inlet * row_values

        def forward_step(running, elements):
            running = elements[0] * running + elements[1]
            return (running, running)
        zero_state = jnp.zeros((R,), jnp.float32)
        _, states = lax.scan(forward_step, zero_state, (carry_mul, drive_term))
        grad_in = out_grads.astype(jnp.float32) * loss_mask
        next_mul = jnp.concatenate([carry_mul[1:], jnp.zeros((1, R), jnp.float32)], axis=0)

        def backward_step(after_grad, elements):
            current = elements[1] + elements[0] * after_grad
            return (current, current)
        _, state_grad = lax.scan(backward_step, zero_state, (next_mul, grad_in), reverse=True)
        prior_state = jnp.concatenate([jnp.zeros((1, R), jnp.float32), states[:-1]], axis=0)
        through = state_grad * gate_inlet * row_values
        grad_log = carry_mul * prior_state * state_grad - keep_mask * through * decay_factor * decay_factor / input_scale
        grad_rate = (grad_log * (-SHARP * soft_decay) * gate_rate * (1.0 - gate_rate)).astype(jnp.bfloat16)
        grad_inlet = (through * input_scale * (1.0 - gate_inlet)).astype(jnp.bfloat16)
        direct = state_grad * input_scale * gate_inlet
        row_grads = (direct + head_back(grad_rate, gate_a) + head_back(grad_inlet, gate_x)).astype(jnp.bfloat16)
        weight_rate = head_outer(token_rows, grad_rate)
        weight_inlet = head_outer(token_rows, grad_inlet)
        decay_grad = SHARP * jax.nn.sigmoid(-decay_param) * lax.optimization_barrier(jnp.sum(grad_log * gate_rate, axis=0))
        return (to_loader(states.astype(jnp.bfloat16), slot_table), to_loader(row_grads, slot_table), weight_rate, weight_inlet, decay_grad)
    outputs = lax.map(one_group, (tokens.reshape(N_DP, GROUP_TOK, R), cotangent.reshape(N_DP, GROUP_TOK, R), arrival_slot, valid_count, doc_lengths))
    return (outputs[0].reshape(TOKENS, R), outputs[1].reshape(TOKENS, R), lax.optimization_barrier(jnp.sum(outputs[2], axis=0)), lax.optimization_barrier(jnp.sum(outputs[3], axis=0)), lax.optimization_barrier(jnp.sum(outputs[4], axis=0)))
```

```python
import functools

import jax
import jax.numpy as jnp
from jax import lax
from jax.experimental import pallas as pl
from jax.experimental.pallas import tpu as pltpu
from jax.sharding import PartitionSpec as P

HS = 320
PAIR = 2 * HS
SHARP = 8.0
TOK = 256
EW = 32
F32 = jnp.float32
BF16 = jnp.bfloat16


def nt_dot(a, b):
    return lax.dot_general(a, b, (((1,), (1,)), ((), ())), preferred_element_type=F32)


def tn_dot(a, b):
    return lax.dot_general(a, b, (((0,), (0,)), ((), ())), preferred_element_type=F32)


def block_diag(w_ref, gate, out_ref):
    lane = lax.broadcasted_iota(jnp.int32, (1, PAIR), 1)
    first = jnp.where(lane < HS, 1.0, 0.0).astype(BF16)
    second = jnp.where(lane < HS, 0.0, 1.0).astype(BF16)
    packed = w_ref[pl.ds(gate * HS, HS), :]
    out_ref[pl.ds(0, HS), :] = packed * first
    out_ref[pl.ds(HS, HS), :] = packed * second


def fill_masks(seq, meta, table, counts, lengths, half, keep_ref, loss_ref):
    block = TOK // seq
    loader = 2 * meta[1] + (meta[2] + half) % 2
    ndoc = lengths.shape[0]
    starts = [jnp.int32(0)]
    for doc in range(ndoc - 1):
        starts.append(starts[-1] + lengths[doc])

    def one(k, carry):
        base = table[loader, k] * block
        inner = base + lax.broadcasted_iota(jnp.int32, (block, 128), 0)
        position = k * TOK + inner
        hit = position == starts[0]
        for start in starts[1:]:
            hit = jnp.logical_or(hit, position == start)
        rows = pl.ds(pl.multiple_of(k * block, block), block)
        keep_ref[rows, :] = jnp.where(hit, 0.0, 1.0)
        if loss_ref is not None:
            loss_ref[rows, :] = jnp.where(inner < counts[k], 1.0, 0.0)
        return carry

    lax.fori_loop(0, seq, one, 0)


def decay_terms(rate, soft, keep):
    u = (2.0 * SHARP) * rate * soft
    decay = jnp.exp(-0.5 * u)
    series = 1.0 - u * (1.0 / 6.0)
    series = 1.0 - u * (1.0 / 5.0) * series
    series = 1.0 - u * (1.0 / 4.0) * series
    series = 1.0 - u * (1.0 / 3.0) * series
    series = 1.0 - u * (1.0 / 2.0) * series
    power = jnp.maximum(u * series, 1e-37)
    inverse = lax.rsqrt(power)
    scale = keep * (power * inverse) + (1.0 - keep)
    return decay, inverse, scale


def wide(column):
    return jnp.concatenate([column] * (PAIR // 128), axis=1)


def put(ref, start, value):
    for tile in range(PAIR // 128):
        rows = pl.ds(pl.multiple_of(tile * TOK + start, EW), EW)
        ref[rows, :] = value[:, tile * 128:(tile + 1) * 128]


def get(ref, start):
    return jnp.concatenate(
        [
            ref[pl.ds(pl.multiple_of(tile * TOK + start, EW), EW), :]
            for tile in range(PAIR // 128)
        ],
        axis=1,
    )


def spread(value, seq):
    return jnp.concatenate([value[:, t * 128:(t + 1) * 128] for t in range(PAIR // 128)], axis=0)


def gather(value, seq):
    return jnp.concatenate([value[t * seq:(t + 1) * seq, :] for t in range(PAIR // 128)], axis=1)


def first_kernel(
    seq, meta, table, counts, lengths,
    xo_ref, xp_ref, go_ref, gp_ref, w_ref, aux_ref,
    rate_ref, inlet_ref, map_ref,
    wa_ref, wx_ref, keep_ref, loss_ref, za_ref, zx_ref, mul_ref, drive_ref, grad_ref,
):
    block = TOK // seq
    block_diag(w_ref, 0, wa_ref)
    block_diag(w_ref, 1, wx_ref)
    soft = aux_ref[0:1, :]
    for half in range(2):
        x_ref = (xo_ref, xp_ref)[half]
        g_ref = (go_ref, gp_ref)[half]
        fill_masks(seq, meta, table, counts, lengths, half, keep_ref, loss_ref)
        za_ref[...] = nt_dot(x_ref[...], wa_ref[...])
        zx_ref[...] = nt_dot(x_ref[...], wx_ref[...])

        def element(i, carry):
            rows = pl.ds(pl.multiple_of(i * EW, EW), EW)
            keep = wide(keep_ref[rows, :])
            rate = jax.nn.sigmoid(za_ref[rows, :])
            inlet = jax.nn.sigmoid(zx_ref[rows, :])
            out_rows = pl.ds(pl.multiple_of(half * TOK + i * EW, EW), EW)
            rate_ref[out_rows, :] = rate
            inlet_ref[out_rows, :] = inlet
            decay, _, scale = decay_terms(rate, soft, keep)
            put(mul_ref, i * EW, keep * decay)
            put(drive_ref, i * EW, scale * inlet * x_ref[rows, :].astype(F32))
            put(grad_ref, i * EW, g_ref[rows, :].astype(F32) * wide(loss_ref[rows, :]))
            return carry

        lax.fori_loop(0, TOK // EW, element, 0)
        count = PAIR // 128 * seq
        prod = jnp.ones((count, 128), F32)
        state = jnp.zeros((count, 128), F32)
        for r in range(block):
            rows = pl.ds(r, count, stride=block)
            mul = mul_ref[rows, :]
            prod = prod * mul
            state = mul * state + drive_ref[rows, :]
        back = jnp.zeros((count, 128), F32)
        for r in reversed(range(block)):
            rows = pl.ds(r, count, stride=block)
            back = mul_ref[rows, :] * (grad_ref[rows, :] + back)
        map_ref[pl.ds(half * seq, seq), :] = gather(prod, seq)
        map_ref[pl.ds((2 + half) * seq, seq), :] = gather(state, seq)
        map_ref[pl.ds((4 + half) * seq, seq), :] = gather(back, seq)


def second_kernel(
    seq, own, meta, table, counts, lengths, *refs
):
    chips = seq // 2
    block = TOK // seq
    map_refs = refs[:chips]
    (xo_ref, xp_ref, go_ref, gp_ref, w_ref, aux_ref, rate_ref, inlet_ref,
     so_ref, sp_ref, to_ref, tp_ref, dw_ref,
     inverse_table, maps, in_state, in_grad, wa_ref, wx_ref, keep_ref, loss_ref,
     mul_ref, drive_ref, grad_ref, carried_ref, dgrad_ref, ga_ref, gx_ref, direct_ref,
     sum_ref, acc_ref) = refs[chips:]
    each = 6 * seq
    for i in range(chips):
        maps[pl.ds(i * each, each), :] = map_refs[i][...]

    def invert(n, carry):
        s, k = n // seq, n % seq
        inverse_table[k, table[s, k]] = s
        return carry

    lax.fori_loop(0, seq * seq, invert, 0)

    def place(p):
        k, q = p // seq, p % seq
        s = inverse_table[k, q]
        chip = jnp.bitwise_xor(s // 2, meta[1])
        half = jnp.bitwise_xor(s % 2, meta[2])
        return chip * each + half * seq + k, (chip * 2 + half) * seq + k

    def compose(p, carry):
        state, grad = carry
        row, slot = place(p)
        in_state[pl.ds(slot, 1), :] = state
        state = maps[pl.ds(row, 1), :] * state + maps[pl.ds(row + 2 * seq, 1), :]
        row, slot = place(seq * seq - 1 - p)
        in_grad[pl.ds(slot, 1), :] = grad
        grad = maps[pl.ds(row, 1), :] * grad + maps[pl.ds(row + 4 * seq, 1), :]
        return state, grad

    zero = jnp.zeros((1, PAIR), F32)
    lax.fori_loop(0, seq * seq, compose, (zero, zero))

    block_diag(w_ref, 0, wa_ref)
    block_diag(w_ref, 1, wx_ref)
    soft = aux_ref[0:1, :]
    acc_ref[...] = jnp.zeros_like(acc_ref)
    lane_id = lax.broadcasted_iota(jnp.int32, (1, PAIR), 1)
    for half in range(2):
        x_ref = (xo_ref, xp_ref)[half]
        g_ref = (go_ref, gp_ref)[half]
        s_ref = (so_ref, sp_ref)[half]
        t_ref = (to_ref, tp_ref)[half]
        fill_masks(seq, meta, table, counts, lengths, half, keep_ref, loss_ref)

        def before(i, carry):
            rows = pl.ds(pl.multiple_of(i * EW, EW), EW)
            saved = pl.ds(pl.multiple_of(half * TOK + i * EW, EW), EW)
            keep = wide(keep_ref[rows, :])
            decay, _, scale = decay_terms(rate_ref[saved, :], soft, keep)
            put(mul_ref, i * EW, keep * decay)
            put(drive_ref, i * EW, scale * inlet_ref[saved, :] * x_ref[rows, :].astype(F32))
            put(grad_ref, i * EW, g_ref[rows, :].astype(F32) * wide(loss_ref[rows, :]))
            return carry

        lax.fori_loop(0, TOK // EW, before, 0)
        count = PAIR // 128 * seq
        state = spread(in_state[pl.ds(half * seq, seq), :], seq)
        for r in range(block):
            rows = pl.ds(r, count, stride=block)
            carried = mul_ref[rows, :] * state
            carried_ref[rows, :] = carried
            state = carried + drive_ref[rows, :]
        back = spread(in_grad[pl.ds(half * seq, seq), :], seq)
        for r in reversed(range(block)):
            rows = pl.ds(r, count, stride=block)
            back = grad_ref[rows, :] + back
            dgrad_ref[rows, :] = back
            back = mul_ref[rows, :] * back

        def after(i, carry):
            rows = pl.ds(pl.multiple_of(i * EW, EW), EW)
            saved = pl.ds(pl.multiple_of(half * TOK + i * EW, EW), EW)
            keep = wide(keep_ref[rows, :])
            rate = rate_ref[saved, :]
            inlet = inlet_ref[saved, :]
            decay, inverse, scale = decay_terms(rate, soft, keep)
            carried = get(carried_ref, i * EW)
            dgrad = get(dgrad_ref, i * EW)
            s_ref[rows, :] = (carried + get(drive_ref, i * EW)).astype(BF16)
            gated = dgrad * inlet
            through = gated * x_ref[rows, :].astype(F32)
            grad_log = carried * dgrad - keep * through * (decay * decay) * inverse
            weighted = grad_log * rate
            ga_ref[rows, :] = (weighted * (-SHARP * soft) * (1.0 - rate)).astype(BF16)
            gx_ref[rows, :] = (through * scale * (1.0 - inlet)).astype(BF16)
            direct_ref[rows, :] = gated * scale
            total = weighted[0:8, :]
            for part in range(8, EW, 8):
                total = total + weighted[part:part + 8, :]
            acc_ref[...] += total
            return carry

        lax.fori_loop(0, TOK // EW, after, 0)
        ga = ga_ref[...]
        gx = gx_ref[...]
        t_ref[...] = (
            direct_ref[...]
            + jnp.dot(ga, wa_ref[...], preferred_element_type=F32)
            + jnp.dot(gx, wx_ref[...], preferred_element_type=F32)
        ).astype(BF16)
        x = x_ref[...]
        for gate, grads in ((0, ga), (1, gx)):
            full = tn_dot(grads, x)
            packed = jnp.where(lane_id < HS, full[:HS, :], full[HS:, :])
            rows = pl.ds(gate * HS, HS)
            if half == 0:
                sum_ref[rows, :] = packed
            else:
                dw_ref[rows, :] = (sum_ref[rows, :] + packed).astype(dw_ref.dtype)
    decay_sum = jnp.sum(acc_ref[...], axis=0, keepdims=True) * aux_ref[1:2, :]
    decay_sum = jnp.broadcast_to(decay_sum, (8, PAIR))
    high = decay_sum.astype(dw_ref.dtype)
    low = (decay_sum - high.astype(F32)).astype(dw_ref.dtype)
    dw_ref[pl.ds(PAIR, 16), :] = jnp.concatenate([high.astype(F32), low.astype(F32)], axis=0).astype(
        dw_ref.dtype
    )


def sum_kernel(chips, meta, *refs):
    parts, out_refs, turned = refs[:-chips - 1], refs[-chips - 1:-1], refs[-1]
    total = parts[0][...]
    for part in parts[1:]:
        total = total + part[...].astype(F32)
    turned[...] = total[:PAIR, :].T
    decay_sum = total[PAIR:PAIR + 8, :] + total[PAIR + 8:PAIR + 16, :]
    high = decay_sum.astype(BF16).astype(F32)
    low = decay_sum - high
    tail = jnp.concatenate([high, low], axis=0).astype(BF16)
    rows = PAIR // chips
    for i in range(chips):
        at = jnp.bitwise_xor(meta[1], i) * rows
        out_refs[i][pl.ds(0, rows), :] = turned[pl.ds(pl.multiple_of(at, 8), rows), :].astype(BF16)
        out_refs[i][pl.ds(rows, 16), :] = tail


def last_kernel(*refs):
    parts, (a_ref, x_ref, decay_ref) = refs[:-3], refs[-3:]
    total = parts[0][...].astype(F32)
    for part in parts[1:]:
        total = total + part[...].astype(F32)
    rows = a_ref.shape[0]
    body = total[:rows, :]
    a_ref[...] = body[:, :HS]
    x_ref[...] = pltpu.roll(body, HS, 1)[:, :HS]
    decay_ref[...] = total[rows:rows + 8, :] + total[rows + 8:rows + 16, :]


def shards(tokens, cotangent, arrival_slot, valid_count, doc_lengths, gate_a, gate_x, decay_param):
    seq = lax.axis_size("seq")
    dp = lax.axis_size("dp")
    chips = seq // 2
    at_dp = lax.axis_index("dp")
    at_seq = lax.axis_index("seq")
    core = at_seq % 2
    chip = at_seq // 2
    meta = jnp.stack([at_dp, chip, core]).astype(jnp.int32)
    table = arrival_slot[0]
    counts = valid_count[0]
    lengths = doc_lengths[0]
    channels = tokens.shape[1]
    half_channels = channels // 2
    swap = [(i, i ^ 1) for i in range(seq)]
    over_dp = [[(i, i ^ j) for i in range(dp)] for j in range(dp)]
    over_chip = [[(i, i ^ (2 * j)) for i in range(seq)] for j in range(chips)]
    to_owner = [
        [(2 * z + c, c * chips + (z ^ j)) for z in range(chips) for c in range(2)]
        for j in range(chips)
    ]

    def other_half(array):
        pieces = []
        for b in range(dp):
            lo = array[:, b * 2 * PAIR:b * 2 * PAIR + PAIR]
            hi = array[:, b * 2 * PAIR + PAIR:(b + 1) * 2 * PAIR]
            pieces.append(jnp.where(core == 0, hi, lo))
        return jnp.concatenate(pieces, axis=1)

    weight = jnp.concatenate(
        [
            lax.dynamic_slice_in_dim(gate_a.T, core * PAIR, PAIR, 1),
            lax.dynamic_slice_in_dim(gate_x.T, core * PAIR, PAIR, 1),
        ],
        axis=0,
    )
    weights = [weight] + [lax.ppermute(weight, "dp", over_dp[j]) for j in range(1, dp)]
    tokens_pair = lax.ppermute(other_half(tokens), "seq", swap)
    cotangent_pair = lax.ppermute(other_half(cotangent), "seq", swap)
    aux = jnp.stack([jax.nn.softplus(-decay_param), SHARP * jax.nn.sigmoid(-decay_param)])

    def own_at(j):
        return lambda i, meta, *_: (0, 2 * jnp.bitwise_xor(meta[0], j) + meta[2])

    def pair_at(j):
        return lambda i, meta, *_: (0, jnp.bitwise_xor(meta[0], j))

    def fixed(i, *_):
        return (0, 0)

    vmem = functools.partial(pltpu.VMEM)
    each = 6 * seq
    scalars = (meta, table, counts, lengths)
    maps, rates, inlets = [], [], []
    for j in range(dp):
        rate, inlet, own_map = pl.pallas_call(
            functools.partial(first_kernel, seq),
            grid_spec=pltpu.PrefetchScalarGridSpec(
                num_scalar_prefetch=4,
                grid=(1,),
                in_specs=[
                    pl.BlockSpec((TOK, PAIR), own_at(j)),
                    pl.BlockSpec((TOK, PAIR), pair_at(j)),
                    pl.BlockSpec((TOK, PAIR), own_at(j)),
                    pl.BlockSpec((TOK, PAIR), pair_at(j)),
                    pl.BlockSpec((PAIR, PAIR), fixed),
                    pl.BlockSpec((2, PAIR), own_at(j)),
                ],
                out_specs=[
                    pl.BlockSpec((2 * TOK, PAIR), fixed),
                    pl.BlockSpec((2 * TOK, PAIR), fixed),
                    pl.BlockSpec((each, PAIR), fixed),
                ],
                scratch_shapes=[
                    vmem((PAIR, PAIR), BF16),
                    vmem((PAIR, PAIR), BF16),
                    vmem((TOK, 128), F32),
                    vmem((TOK, 128), F32),
                ] + [vmem((TOK, PAIR), F32)] * 2 + [vmem((PAIR // 128 * TOK, 128), F32)] * 3,
            ),
            out_shape=[
                jax.ShapeDtypeStruct((2 * TOK, PAIR), F32),
                jax.ShapeDtypeStruct((2 * TOK, PAIR), F32),
                jax.ShapeDtypeStruct((each, PAIR), F32),
            ],
            cost_estimate=pl.CostEstimate(
                flops=4 * 2 * TOK * PAIR * PAIR, bytes_accessed=6 << 20, transcendentals=0
            ),
            name="gates",
        )(*scalars, tokens, tokens_pair, cotangent, cotangent_pair, weights[j], aux)
        rates.append(rate)
        inlets.append(inlet)
        maps.append([own_map] + [lax.ppermute(own_map, "seq", over_chip[i]) for i in range(1, chips)])

    states_own, states_pair, grads_own, grads_pair, partials = [], [], [], [], []
    for j in range(dp):
        dtype = F32 if j == 0 else BF16
        tile = pl.BlockSpec((TOK, PAIR), fixed)
        results = pl.pallas_call(
            functools.partial(second_kernel, seq, j == 0),
            grid_spec=pltpu.PrefetchScalarGridSpec(
                num_scalar_prefetch=4,
                grid=(1,),
                in_specs=[pl.BlockSpec((each, PAIR), fixed)] * chips + [
                    pl.BlockSpec((TOK, PAIR), own_at(j)),
                    pl.BlockSpec((TOK, PAIR), pair_at(j)),
                    pl.BlockSpec((TOK, PAIR), own_at(j)),
                    pl.BlockSpec((TOK, PAIR), pair_at(j)),
                    pl.BlockSpec((PAIR, PAIR), fixed),
                    pl.BlockSpec((2, PAIR), own_at(j)),
                    pl.BlockSpec((2 * TOK, PAIR), fixed),
                    pl.BlockSpec((2 * TOK, PAIR), fixed),
                ],
                out_specs=[tile, tile, tile, tile, pl.BlockSpec((PAIR + 16, PAIR), fixed)],
                scratch_shapes=[
                    pltpu.SMEM((seq, seq), jnp.int32),
                    vmem((chips * each, PAIR), F32),
                    vmem((seq * seq, PAIR), F32),
                    vmem((seq * seq, PAIR), F32),
                    vmem((PAIR, PAIR), BF16),
                    vmem((PAIR, PAIR), BF16),
                    vmem((TOK, 128), F32),
                    vmem((TOK, 128), F32),
                ] + [vmem((PAIR // 128 * TOK, 128), F32)] * 5 + [
                    vmem((TOK, PAIR), BF16),
                    vmem((TOK, PAIR), BF16),
                    vmem((TOK, PAIR), F32),
                    vmem((PAIR, PAIR), F32),
                    vmem((8, PAIR), F32),
                ],
            ),
            out_shape=[jax.ShapeDtypeStruct((TOK, PAIR), BF16)] * 4
            + [jax.ShapeDtypeStruct((PAIR + 16, PAIR), dtype)],
            cost_estimate=pl.CostEstimate(
                flops=8 * 2 * TOK * PAIR * PAIR, bytes_accessed=8 << 20, transcendentals=0
            ),
            name="grads",
        )(*scalars, *maps[j], tokens, tokens_pair, cotangent, cotangent_pair, weights[j], aux,
          rates[j], inlets[j])
        states_own.append(results[0])
        states_pair.append(results[1])
        grads_own.append(results[2])
        grads_pair.append(results[3])
        partials.append(results[4] if j == 0 else lax.ppermute(results[4], "dp", over_dp[j]))

    rows = PAIR // chips
    whole = pl.BlockSpec(memory_space=pltpu.VMEM)
    messages = pl.pallas_call(
        functools.partial(sum_kernel, chips),
        in_specs=[pl.BlockSpec(memory_space=pltpu.SMEM)] + [whole] * dp,
        out_specs=[whole] * chips,
        scratch_shapes=[vmem((PAIR, PAIR), F32)],
        out_shape=[jax.ShapeDtypeStruct((rows + 16, PAIR), BF16)] * chips,
        name="sums",
    )(meta, *partials)
    arrived = [lax.ppermute(messages[j], "seq", to_owner[j]) for j in range(chips)]
    part_rate, part_inlet, decay_rows = pl.pallas_call(
        last_kernel,
        in_specs=[whole] * chips,
        out_specs=[whole] * 3,
        out_shape=[
            jax.ShapeDtypeStruct((rows, HS), F32),
            jax.ShapeDtypeStruct((rows, HS), F32),
            jax.ShapeDtypeStruct((8, PAIR), F32),
        ],
        name="totals",
    )(*arrived)
    part_decay = lax.dynamic_slice_in_dim(decay_rows[0], (at_seq % chips) * rows, rows)

    def assemble(own, pair):
        def in_order(parts):
            ordered = []
            for b in range(dp):
                value = parts[0]
                for j in range(1, dp):
                    value = jnp.where(at_dp == (b ^ j), parts[j], value)
                ordered.append(value)
            return ordered

        arrived = [lax.ppermute(part, "seq", swap) for part in pair]
        pieces = []
        for mine, theirs in zip(in_order(own), in_order(arrived)):
            pieces.append(jnp.where(core == 0, mine, theirs))
            pieces.append(jnp.where(core == 0, theirs, mine))
        return jnp.concatenate(pieces, axis=1)

    return (
        assemble(states_own, states_pair),
        assemble(grads_own, grads_pair),
        part_rate,
        part_inlet,
        part_decay,
    )


def solution(mesh):
    return jax.shard_map(
        shards,
        mesh=mesh,
        in_specs=(
            P(("dp", "seq"), None),
            P(("dp", "seq"), None),
            P("dp", None, None),
            P("dp", None),
            P("dp", None),
            P("dp", None),
            P("dp", None),
            P(),
        ),
        out_specs=(
            P(("dp", "seq"), None),
            P(("dp", "seq"), None),
            P(("dp", "seq"), None),
            P(("dp", "seq"), None),
            P(("dp", "seq")),
        ),
        check_vma=False,
    )
```

```python
import functools

import jax
import jax.numpy as jnp
from jax import lax
from jax.experimental import pallas as pl
from jax.experimental.pallas import tpu as pltpu
from jax.sharding import PartitionSpec as P


HS = 320
PAIR = 2 * HS
SHARP = 8.0
TOK = 256
EW = 32
F32 = jnp.float32
BF16 = jnp.bfloat16


def nt_dot(a, b):
    return lax.dot_general(a, b, (((1,), (1,)), ((), ())), preferred_element_type=F32)


def tn_dot(a, b):
    return lax.dot_general(a, b, (((0,), (0,)), ((), ())), preferred_element_type=F32)


def block_diag(w_refs, gate, out_ref):
    lane = lax.broadcasted_iota(jnp.int32, (1, PAIR), 1)
    first = jnp.where(lane < HS, 1.0, 0.0).astype(BF16)
    second = jnp.where(lane < HS, 0.0, 1.0).astype(BF16)
    packed = w_refs[gate][...] if len(w_refs) == 2 else w_refs[0][pl.ds(gate * HS, HS), :]
    out_ref[pl.ds(0, HS), :] = packed * first
    out_ref[pl.ds(HS, HS), :] = packed * second


def piece_vectors(seq, meta, table, counts, half):
    block = TOK // seq
    loader = 2 * meta[1] + (meta[2] + half) % 2
    piece = lax.broadcasted_iota(jnp.int32, (seq, 128), 0)
    base = jnp.zeros((seq, 128), jnp.int32)
    limit = jnp.zeros((seq, 128), jnp.int32)
    for k in range(seq):
        here = piece == k
        base = jnp.where(here, k * TOK + table[loader, k] * block, base)
        limit = jnp.where(here, k * TOK + counts[k], limit)
    return base, limit


def gates_kernel(seq, parts, meta, table, counts, lengths, order, *refs):
    w_refs = refs[:parts]
    (xo_ref, xp_ref, go_ref, gp_ref, aux_ref, perm_ref,
     x_ref, g_ref, rate_ref, mul_ref, drive_ref, carry_ref, direct_ref, inward_ref, map_ref,
     wa_ref, wx_ref, za_ref, zx_ref) = refs[parts:]
    block = TOK // seq
    steps = EW // seq
    block_diag(w_refs, 0, wa_ref)
    block_diag(w_refs, 1, wx_ref)
    starts = [jnp.int32(0)]
    for doc in range(lengths.shape[0] - 1):
        starts.append(starts[-1] + lengths[doc])
    perm = perm_ref[0:TOK, :]
    for half in range(2):
        rows = pl.ds(half * TOK, TOK)
        x_ref[rows, :] = jnp.dot(
            perm, (xo_ref, xp_ref)[half][...], preferred_element_type=F32
        ).astype(BF16)
        za_ref[rows, :] = jnp.dot(
            perm, (go_ref, gp_ref)[half][...], preferred_element_type=F32
        )
    for half in range(2):
        base, limit = piece_vectors(seq, meta, table, counts, half)

        def mask(i, carry):
            rows = pl.ds(pl.multiple_of(half * TOK + i * EW, EW), EW)
            used = []
            for e in range(steps):
                used.append(jnp.where(base + (i * steps + e) < limit, 1.0, 0.0))
            used = jnp.concatenate(used, axis=0)
            for tile in range(PAIR // 128):
                lanes = slice(tile * 128, (tile + 1) * 128)
                g_ref[rows, lanes] = (za_ref[rows, lanes] * used).astype(BF16)
            return carry

        lax.fori_loop(0, TOK // EW, mask, 0)
    za_ref[...] = nt_dot(x_ref[...], wa_ref[...])
    zx_ref[...] = nt_dot(x_ref[...], wx_ref[...])
    for half in range(2):
        base, _ = piece_vectors(seq, meta, table, counts, half)

        def element(i, carry):
            rows = pl.ds(pl.multiple_of(half * TOK + i * EW, EW), EW)
            first = []
            for e in range(steps):
                position = base + (i * steps + e)
                hit = position == starts[0]
                for start in starts[1:]:
                    hit = jnp.logical_or(hit, position == start)
                first.append(jnp.where(hit, 1.0, 0.0))
            first = jnp.concatenate(first, axis=0)
            keep = 1.0 - first
            for tile in range(PAIR // 128):
                lanes = slice(tile * 128, (tile + 1) * 128)
                rate = jax.nn.sigmoid(za_ref[rows, lanes])
                inlet = jax.nn.sigmoid(zx_ref[rows, lanes])
                u = rate * ((2.0 * SHARP) * aux_ref[0:1, lanes])
                decay = jnp.exp(-0.5 * u)
                series = u * (-1.0 / 720.0) + (1.0 / 120.0)
                series = u * series - (1.0 / 24.0)
                series = u * series + (1.0 / 6.0)
                series = u * series - 0.5
                series = u * series + 1.0
                power = jnp.maximum(u * series, 1e-37)
                inverse = lax.rsqrt(power)
                scale = keep * (power * inverse) + first
                factor = scale * inlet
                value = inlet * x_ref[rows, lanes].astype(F32)
                drive = scale * value
                rate_ref[rows, lanes] = rate
                mul_ref[rows, lanes] = keep * decay
                drive_ref[rows, lanes] = drive
                carry_ref[rows, lanes] = (keep * inverse) * (decay * decay) * value
                direct_ref[rows, lanes] = factor
                inward_ref[rows, lanes] = drive - drive * inlet
            return carry

        lax.fori_loop(0, TOK // EW, element, 0)
        prod = jnp.ones((seq, PAIR), F32)
        state = jnp.zeros((seq, PAIR), F32)
        for r in range(block):
            rows = pl.ds(half * TOK + r * seq, seq)
            mul = mul_ref[rows, :]
            prod = prod * mul
            state = mul * state + drive_ref[rows, :]
        back = jnp.zeros((seq, PAIR), F32)
        for r in reversed(range(0, block, 2)):
            grads = g_ref[pl.ds(half * TOK + r * seq, 2 * seq), :].astype(F32)
            for e in (1, 0):
                rows = pl.ds(half * TOK + (r + e) * seq, seq)
                back = mul_ref[rows, :] * (grads[e * seq:(e + 1) * seq, :] + back)
        map_ref[pl.ds(half * seq, seq), :] = prod
        map_ref[pl.ds((2 + half) * seq, seq), :] = state
        map_ref[pl.ds((4 + half) * seq, seq), :] = back


def grads_kernel(seq, parts, meta, table, counts, lengths, order, *refs):
    chips = seq // 2
    w_refs, refs = refs[:parts], refs[parts:]
    block = TOK // seq
    map_refs = refs[:chips]
    (x_ref, g_ref, rate_ref, mul_ref, drive_ref, carry_ref, direct_ref, inward_ref,
     aux_ref, perm_ref,
     so_ref, sp_ref, to_ref, tp_ref, dw_ref,
     maps, in_state, in_grad, wa_ref, wx_ref,
     carried_ref, dgrad_ref, ga_ref, gx_ref, st_ref, acc_ref) = refs[chips:]
    each = 6 * seq
    for i in range(chips):
        maps[pl.ds(i * each, each), :] = map_refs[i][...]
    count = seq * seq
    unroll = 8

    def compose(group, carry):
        state, grad = carry
        for e in range(unroll):
            p = group * unroll + e
            row, slot = order[0, p], order[1, p]
            in_state[pl.ds(slot, 1), :] = state
            state = maps[pl.ds(row, 1), :] * state + maps[pl.ds(row + 2 * seq, 1), :]
            back = count - 1 - p
            row, slot = order[0, back], order[1, back]
            in_grad[pl.ds(slot, 1), :] = grad
            grad = maps[pl.ds(row, 1), :] * grad + maps[pl.ds(row + 4 * seq, 1), :]
        return state, grad

    zero = jnp.zeros((1, PAIR), F32)
    lax.fori_loop(0, count // unroll, compose, (zero, zero))
    block_diag(w_refs, 0, wa_ref)
    block_diag(w_refs, 1, wx_ref)
    acc_ref[...] = jnp.zeros_like(acc_ref)
    for half in range(2):
        state = in_state[pl.ds(half * seq, seq), :]
        for r in range(block):
            rows = pl.ds(half * TOK + r * seq, seq)
            carried = mul_ref[rows, :] * state
            carried_ref[rows, :] = carried
            state = carried + drive_ref[rows, :]
        back = in_grad[pl.ds(half * seq, seq), :]
        for r in reversed(range(0, block, 2)):
            grads = g_ref[pl.ds(half * TOK + r * seq, 2 * seq), :].astype(F32)
            for e in (1, 0):
                rows = pl.ds(half * TOK + (r + e) * seq, seq)
                back = grads[e * seq:(e + 1) * seq, :] + back
                dgrad_ref[rows, :] = back
                back = mul_ref[rows, :] * back

    def after(i, carry):
        rows = pl.ds(pl.multiple_of(i * EW, EW), EW)
        for tile in range(PAIR // 128):
            lanes = slice(tile * 128, (tile + 1) * 128)
            rate = rate_ref[rows, lanes]
            carried = carried_ref[rows, lanes]
            dgrad = dgrad_ref[rows, lanes]
            st_ref[rows, lanes] = (carried + drive_ref[rows, lanes]).astype(BF16)
            weighted = dgrad * (carried - carry_ref[rows, lanes]) * rate
            ga_ref[rows, lanes] = (
                (weighted - weighted * rate) * (-SHARP * aux_ref[0:1, lanes])
            ).astype(BF16)
            gx_ref[rows, lanes] = (dgrad * inward_ref[rows, lanes]).astype(BF16)
            dgrad_ref[rows, lanes] = dgrad * direct_ref[rows, lanes]
            total = weighted[0:8, :]
            for part in range(8, EW, 8):
                total = total + weighted[part:part + 8, :]
            acc_ref[:, lanes] += total
        return carry

    lax.fori_loop(0, 2 * TOK // EW, after, 0)
    ga = ga_ref[...]
    gx = gx_ref[...]
    turned = (
        dgrad_ref[...]
        + jnp.dot(ga, wa_ref[...], preferred_element_type=F32)
        + jnp.dot(gx, wx_ref[...], preferred_element_type=F32)
    ).astype(BF16)
    back_perm = perm_ref[TOK:2 * TOK, :]
    for half in range(2):
        part = slice(half * TOK, (half + 1) * TOK)
        (so_ref, sp_ref)[half][...] = jnp.dot(
            back_perm, st_ref[part, :], preferred_element_type=F32
        ).astype(BF16)
        (to_ref, tp_ref)[half][...] = jnp.dot(
            back_perm, turned[part, :], preferred_element_type=F32
        ).astype(BF16)
    lane_id = lax.broadcasted_iota(jnp.int32, (1, PAIR), 1)
    x = x_ref[...]
    for gate, grads in ((0, ga), (1, gx)):
        full = tn_dot(grads, x)
        dw_ref[pl.ds(gate * HS, HS), :] = jnp.where(
            lane_id < HS, full[:HS, :], full[HS:, :]
        ).astype(dw_ref.dtype)
    decay_sum = jnp.sum(acc_ref[...], axis=0, keepdims=True) * aux_ref[1:2, :]
    decay_sum = jnp.broadcast_to(decay_sum, (8, PAIR))
    high = decay_sum.astype(dw_ref.dtype)
    low = (decay_sum - high.astype(F32)).astype(dw_ref.dtype)
    dw_ref[pl.ds(PAIR, 16), :] = jnp.concatenate([high.astype(F32), low.astype(F32)], axis=0).astype(
        dw_ref.dtype
    )


def sum_kernel(chips, meta, *refs):
    parts, out_refs, turned = refs[:-chips - 1], refs[-chips - 1:-1], refs[-1]
    total = parts[0][...]
    for part in parts[1:]:
        total = total + part[...].astype(F32)
    turned[...] = total[:PAIR, :].T
    decay_sum = total[PAIR:PAIR + 8, :] + total[PAIR + 8:PAIR + 16, :]
    high = decay_sum.astype(BF16).astype(F32)
    low = decay_sum - high
    tail = jnp.concatenate([high, low], axis=0).astype(BF16)
    rows = PAIR // chips
    for i in range(chips):
        at = jnp.bitwise_xor(meta[1], i) * rows
        out_refs[i][pl.ds(0, rows), :] = turned[pl.ds(pl.multiple_of(at, 8), rows), :].astype(BF16)
        out_refs[i][pl.ds(rows, 16), :] = tail


def last_kernel(*refs):
    parts, (a_ref, x_ref, decay_ref) = refs[:-3], refs[-3:]
    total = parts[0][...].astype(F32)
    for part in parts[1:]:
        total = total + part[...].astype(F32)
    rows = a_ref.shape[0]
    body = total[:rows, :]
    a_ref[...] = body[:, :HS]
    x_ref[...] = pltpu.roll(body, HS, 1)[:, :HS]
    decay_ref[...] = total[rows:rows + 8, :] + total[rows + 8:rows + 16, :]


def shards(tokens, cotangent, arrival_slot, valid_count, doc_lengths, gate_a, gate_x, decay_param):
    seq = lax.axis_size("seq")
    dp = lax.axis_size("dp")
    chips = seq // 2
    at_dp = lax.axis_index("dp")
    at_seq = lax.axis_index("seq")
    core = at_seq % 2
    chip = at_seq // 2
    steps = [0, 1 + core, 2 - core, 3]
    blocks = [jnp.bitwise_xor(at_dp, step) for step in steps]
    meta = jnp.stack([at_dp, chip, core] + blocks).astype(jnp.int32)
    table = arrival_slot[0]
    counts = valid_count[0]
    lengths = doc_lengths[0]
    swap = [(i, i ^ 1) for i in range(seq)]
    flat = [(d, s) for d in range(dp) for s in range(seq)]
    hops = [
        [(d * seq + s, (d ^ (1 + s % 2 if kind == 1 else 2 - s % 2)) * seq + s) for d, s in flat]
        for kind in (1, 2)
    ]
    across = [(d * seq + s, (d ^ 3) * seq + s) for d, s in flat]
    mesh_axes = ("dp", "seq")
    over_chip = [[(i, i ^ (2 * j)) for i in range(seq)] for j in range(chips)]
    to_owner = [
        [(2 * z + c, c * chips + (z ^ j)) for z in range(chips) for c in range(2)]
        for j in range(chips)
    ]

    def other_half(array):
        pieces = []
        for b in range(dp):
            lo = array[:, b * 2 * PAIR:b * 2 * PAIR + PAIR]
            hi = array[:, b * 2 * PAIR + PAIR:(b + 1) * 2 * PAIR]
            pieces.append(jnp.where(core == 0, hi, lo))
        return jnp.concatenate(pieces, axis=1)

    weight = jnp.concatenate(
        [
            lax.dynamic_slice_in_dim(gate_a.T, core * PAIR, PAIR, 1),
            lax.dynamic_slice_in_dim(gate_x.T, core * PAIR, PAIR, 1),
        ],
        axis=0,
    )
    near = lax.ppermute(weight, mesh_axes, hops[0])
    next_near = lax.ppermute(weight, mesh_axes, hops[1])
    far = (
        lax.ppermute(next_near[:HS], mesh_axes, hops[0]),
        lax.ppermute(near[HS:], mesh_axes, hops[1]),
    )
    weights = [(weight,), (near,), (next_near,), far]
    tokens_pair = lax.ppermute(other_half(tokens), "seq", swap)
    cotangent_pair = lax.ppermute(other_half(cotangent), "seq", swap)
    aux = jnp.stack([jax.nn.softplus(-decay_param), SHARP * jax.nn.sigmoid(-decay_param)])

    def own_at(j):
        return lambda i, meta, *_: (0, 2 * meta[3 + j] + meta[2])

    def pair_at(j):
        return lambda i, meta, *_: (0, meta[3 + j])

    vmem = pltpu.VMEM
    each = 6 * seq
    block = TOK // seq
    piece = jnp.arange(seq, dtype=jnp.int32)
    found = jnp.sum(
        jnp.where(table[:, :, None] == piece[None, None, :], piece[:, None, None], 0), axis=0
    )
    chip_at = jnp.bitwise_xor(found // 2, chip)
    half_at = jnp.bitwise_xor(found % 2, core)
    place = half_at * seq + piece[:, None]
    order = jnp.stack(
        [(chip_at * each + place).reshape(-1), (chip_at * 2 * seq + place).reshape(-1)]
    ).astype(jnp.int32)
    row = jnp.arange(TOK)
    forth = ((row % seq) * block + row // seq)[:, None] == row[None, :]
    perm = jnp.concatenate([forth, forth.T], axis=0).astype(BF16)
    scalars = (meta, table, counts, lengths, order)
    small = seq <= 8
    limit = (16 << 20) if small else (48 << 20)
    whole = pl.BlockSpec(memory_space=pltpu.VMEM)
    saved = [jax.ShapeDtypeStruct((2 * TOK, PAIR), BF16)] * 2 + [
        jax.ShapeDtypeStruct((2 * TOK, PAIR), F32)
    ] * 6
    maps, kept, results = {}, {}, {}

    def run_gates(j):
        parts = len(weights[j])
        *keeping, own_map = pl.pallas_call(
            functools.partial(gates_kernel, seq, parts),
            grid_spec=pltpu.PrefetchScalarGridSpec(
                num_scalar_prefetch=5,
                grid=(1,),
                in_specs=[whole] * parts + [
                    pl.BlockSpec((TOK, PAIR), own_at(j)),
                    pl.BlockSpec((TOK, PAIR), pair_at(j)),
                    pl.BlockSpec((TOK, PAIR), own_at(j)),
                    pl.BlockSpec((TOK, PAIR), pair_at(j)),
                    pl.BlockSpec((2, PAIR), own_at(j)),
                    whole,
                ],
                out_specs=[whole] * 9,
                scratch_shapes=[
                    vmem((PAIR, PAIR), BF16),
                    vmem((PAIR, PAIR), BF16),
                    vmem((2 * TOK, PAIR), F32),
                    vmem((2 * TOK, PAIR), F32),
                ],
            ),
            out_shape=saved + [jax.ShapeDtypeStruct((each, PAIR), F32)],
            compiler_params=pltpu.CompilerParams(vmem_limit_bytes=limit),
            cost_estimate=pl.CostEstimate(
                flops=4 * 2 * TOK * PAIR * PAIR, bytes_accessed=6 << 20, transcendentals=0
            ),
            name="gates",
        )(*scalars, *weights[j], tokens, tokens_pair, cotangent, cotangent_pair, aux, perm)
        kept[j] = keeping
        maps[j] = [own_map] + [lax.ppermute(own_map, "seq", over_chip[i]) for i in range(1, chips)]

    def run_grads(j):
        parts = len(weights[j])
        dtype = F32 if j == 0 else BF16
        *result, partial = pl.pallas_call(
            functools.partial(grads_kernel, seq, parts),
            grid_spec=pltpu.PrefetchScalarGridSpec(
                num_scalar_prefetch=5,
                grid=(1,),
                in_specs=[whole] * (parts + chips + 8) + [pl.BlockSpec((2, PAIR), own_at(j)), whole],
                out_specs=[whole] * 5,
                scratch_shapes=[
                    vmem((chips * each, PAIR), F32),
                    vmem((seq * seq, PAIR), F32),
                    vmem((seq * seq, PAIR), F32),
                    vmem((PAIR, PAIR), BF16),
                    vmem((PAIR, PAIR), BF16),
                    vmem((2 * TOK, PAIR), F32),
                    vmem((2 * TOK, PAIR), F32),
                    vmem((2 * TOK, PAIR), BF16),
                    vmem((2 * TOK, PAIR), BF16),
                    vmem((2 * TOK, PAIR), BF16),
                    vmem((8, PAIR), F32),
                ],
            ),
            out_shape=[jax.ShapeDtypeStruct((TOK, PAIR), BF16)] * 4
            + [jax.ShapeDtypeStruct((PAIR + 16, PAIR), dtype)],
            compiler_params=pltpu.CompilerParams(vmem_limit_bytes=limit),
            cost_estimate=pl.CostEstimate(
                flops=8 * 2 * TOK * PAIR * PAIR, bytes_accessed=8 << 20, transcendentals=0
            ),
            name="grads",
        )(*scalars, *weights[j], *maps[j], *kept[j], aux, perm)
        if j:
            pairs = across if j == 3 else hops[j - 1]
            partial = lax.ppermute(partial, mesh_axes, pairs)
        results[j] = (*result, partial)

    for j in range(4):
        run_gates(j)
    for j in range(4):
        run_grads(j)
    states_own, states_pair, grads_own, grads_pair, partials = zip(*(results[j] for j in range(4)))

    rows = PAIR // chips
    messages = pl.pallas_call(
        functools.partial(sum_kernel, chips),
        in_specs=[pl.BlockSpec(memory_space=pltpu.SMEM)] + [whole] * 4,
        out_specs=[whole] * chips,
        scratch_shapes=[vmem((PAIR, PAIR), F32)],
        out_shape=[jax.ShapeDtypeStruct((rows + 16, PAIR), BF16)] * chips,
        name="sums",
    )(meta, *partials)
    arrived = [lax.ppermute(messages[j], "seq", to_owner[j]) for j in range(chips)]
    part_rate, part_inlet, decay_rows = pl.pallas_call(
        last_kernel,
        in_specs=[whole] * chips,
        out_specs=[whole] * 3,
        out_shape=[
            jax.ShapeDtypeStruct((rows, HS), F32),
            jax.ShapeDtypeStruct((rows, HS), F32),
            jax.ShapeDtypeStruct((8, PAIR), F32),
        ],
        name="totals",
    )(*arrived)
    part_decay = lax.dynamic_slice_in_dim(decay_rows[0], (at_seq % chips) * rows, rows)

    def assemble(own, pair):
        def in_order(parts, blocks):
            ordered = []
            for b in range(dp):
                value = parts[0]
                for j in range(1, 4):
                    value = jnp.where(blocks[j] == b, parts[j], value)
                ordered.append(value)
            return ordered

        arrived = [lax.ppermute(part, "seq", swap) for part in pair]
        pieces = []
        theirs_at = [blocks[0], blocks[2], blocks[1], blocks[3]]
        for mine, theirs in zip(in_order(own, blocks), in_order(arrived, theirs_at)):
            pieces.append(jnp.where(core == 0, mine, theirs))
            pieces.append(jnp.where(core == 0, theirs, mine))
        return jnp.concatenate(pieces, axis=1)

    return (
        assemble(states_own, states_pair),
        assemble(grads_own, grads_pair),
        part_rate,
        part_inlet,
        part_decay,
    )


def solution(mesh):
    return jax.shard_map(
        shards,
        mesh=mesh,
        in_specs=(
            P(("dp", "seq"), None),
            P(("dp", "seq"), None),
            P("dp", None, None),
            P("dp", None),
            P("dp", None),
            P("dp", None),
            P("dp", None),
            P(),
        ),
        out_specs=(
            P(("dp", "seq"), None),
            P(("dp", "seq"), None),
            P(("dp", "seq"), None),
            P(("dp", "seq"), None),
            P(("dp", "seq")),
        ),
        check_vma=False,
    )
```
